32 devices in a mesh: row: 8 (over z, core), col: 4 (over y, x).
Axes of the slice: x: 2, y: 2, z: 4, core: 2. Of those that a mesh axis runs over, the one named last changes fastest.
Arguments:
- gram: bfloat16 [32768, 32768], P('row', 'col'), may hold values from -1 to 5, as said below
- start_basis: bfloat16 [32768, 256], P(('row', 'col')), may hold values from -12 to 12
- slab: float32 [32768, 4096], P('row', 'col'), may hold values from -6 to 6
Outputs:
- core_scaled: float32 [32768, 256], P(('row', 'col'))
- next_unfolding: float32 [4096, 256], P(('row', 'col'))
The draws below stay inside these ranges and needn't reach their ends.
Inputs may be any that keep to these rules, and one draw needn't show every extreme that they name: gram is symmetric: entry (i, j) equals entry (j, i).
All inputs are finite; a program needn't handle non-finite values.
Results may differ from the reference program's by a relative error of at most 0.003.
Values may be sent and summed in bfloat16 or wider, within the bound.
A program may use at most 192 MiB of HBM per device.

```python
import math
import jax
import jax.numpy as jnp
from jax import lax

N = 32768
P_SIZE = 256
NMODE = 16
REST = 256
W = 4096


def draw_gram(key, part):
    span = math.gcd(N, 512)
    blocks = N // span
    off_scale = 0.3 / math.sqrt(N)
    position = jnp.arange(N, dtype=jnp.float32) / N
    spread = 1.8
    factors = jnp.exp(jax.random.uniform(jax.random.fold_in(key, 12), (N,), minval=0.0, maxval=math.log(spread)))
    diagonal = 0.5 * jnp.exp(position * math.log(3.0)) * factors
    tile_key = jax.random.fold_in(key, 11)

    def one_tile(row_block, col_block):
        lesser = jnp.minimum(row_block, col_block)
        greater = jnp.maximum(row_block, col_block)
        sub_key = jax.random.fold_in(tile_key, lesser * blocks + greater)
        base = jnp.clip(jax.random.normal(sub_key, (span, span)), -6.0, 6.0)
        mirror = base.T
        tile = jnp.where(row_block < col_block, base, jnp.where(row_block > col_block, mirror, (base + mirror) * 0.70710678))
        segment = lax.dynamic_slice_in_dim(diagonal, row_block * span, span, 0)
        on_diag = jnp.where(row_block == col_block, 1.0, 0.0)
        return tile * off_scale + on_diag * jnp.diag(segment)

    def block_row(row_block):
        tiles = jax.vmap(lambda col_block: one_tile(row_block, col_block))(jnp.arange(blocks))
        return tiles.astype(jnp.bfloat16)
    stacked = lax.map(block_row, jnp.arange(blocks))
    return stacked.transpose(0, 2, 1, 3).reshape(N, N)


def draw_start_basis(key, part):
    scale_key, main_key = jax.random.split(jax.random.fold_in(key, 21), 2)
    scales = jnp.exp(jax.random.uniform(scale_key, (P_SIZE,), minval=math.log(0.3), maxval=math.log(3.0)))
    base = jnp.clip(jax.random.normal(main_key, (N, P_SIZE)), -6.0, 6.0)
    return jnp.clip(base * scales[None, :], -12.0, 12.0).astype(jnp.bfloat16)


def block_scale(rng, dims, cuts, least, high):
    loudness = 1.0
    for dim, shards_of in cuts:
        draws = jax.random.uniform(jax.random.fold_in(jax.random.fold_in(rng, 6), dim), (shards_of,), jnp.float32, least / len(cuts), high / len(cuts))
        loudness = loudness * jnp.repeat(jnp.exp(draws), dims[dim] // shards_of).reshape((-1,) + (1,) * (len(dims) - 1 - dim))
    return loudness


def noise(key, dims, scale, reach, cuts=(), held_as=jnp.bfloat16):
    values = jax.random.normal(key, dims, jnp.float32) * scale
    if len(cuts) > 0:
        values = block_scale(key, dims, cuts, -0.22, 0.18) * values
    return jnp.clip(values, min=-reach, max=reach).astype(held_as)


def setup_inputs(seed: int = 0) -> dict:
    seeds = jax.random.split(jax.random.key(seed), 4)
    return {
        "gram": draw_gram(jax.random.fold_in(seeds[3], 71), 0),
        "start_basis": draw_start_basis(jax.random.fold_in(seeds[3], 71), 0),
        "slab": noise(seeds[2], (N, W), 1.0, 6.0, ((0, 8), (1, 4)), jnp.float32),
    }


def gram_times(gram, source):
    span = math.gcd(N, 4096)
    source_wide = source.astype(jnp.float32)

    def one_block(rows_block):
        return jnp.dot(rows_block.astype(jnp.float32), source_wide, precision=lax.Precision.HIGHEST)
    pieces = lax.map(one_block, gram.reshape(N // span, span, N))
    return pieces.reshape(N, source.shape[1])

def reference(gram, start_basis, slab):
    first_image = gram_times(gram, start_basis).astype(jnp.bfloat16)
    second_image = gram_times(gram, first_image)
    small_gram = jnp.dot(second_image.T, second_image, precision=lax.Precision.HIGHEST)
    factor = jnp.linalg.cholesky(small_gram)
    basis_cols = jax.scipy.linalg.solve_triangular(factor, second_image.T, lower=True).T
    core_scaled = basis_cols * math.sqrt(N)
    projection = jnp.dot(basis_cols.T, slab, precision=lax.Precision.HIGHEST)
    next_unfolding = projection.reshape(P_SIZE * NMODE, REST)
    return (core_scaled, next_unfolding)
```

```python
import functools
import math

import jax
import jax.numpy as jnp
from jax import lax
from jax.experimental import pallas as pl
from jax.experimental.pallas import tpu as pltpu
from jax.sharding import PartitionSpec as P

HIGHEST = lax.Precision.HIGHEST
CONTRACT_ROWS = (((0,), (0,)), ((), ()))
MESH = pl.DeviceIdType.MESH


def far_first(z, planes, i):
    below, above = z, planes - 1 - z
    less, more = jnp.minimum(below, above), jnp.maximum(below, above)
    lone = i < more - less
    rest = i - (more - less)
    distance = jnp.where(lone, more - i, less - lax.div(rest, 2))
    upward = jnp.where(lone, above >= below, lax.rem(rest, 2) == 0)
    return jnp.where(upward, z + distance, z - distance)


def products_kernel(
    rows, cols, chunks, gram, x_ref, out_ref,
    tiles, tile_sem, xs, xs_send, xs_recv,
    both, theirs, pair_send, pair_recv,
    sums, sum_send, sum_recv,
    image, hop_send, hop_recv, mate_send, mate_recv,
):
    planes = rows // 2
    r, c = lax.axis_index("row"), lax.axis_index("col")
    z, core = lax.div(r, 2), lax.rem(r, 2)
    piece, width = x_ref.shape
    w = piece // chunks
    mate = (r + 1 - 2 * core, c)
    upper, lower = (jnp.minimum(r + 2, rows - 1), c), (jnp.maximum(r - 2, 0), c)
    has_up, has_low = z < planes - 1, z > 0
    order = lambda i: far_first(z, planes, i)

    def remote(src, dst, send, recv, to):
        return pltpu.make_async_remote_copy(
            src_ref=src, dst_ref=dst, send_sem=send, recv_sem=recv, device_id=to, device_id_type=MESH
        )

    def fetch(q, d, slot):
        return [
            pltpu.make_async_copy(
                gram.at[:, pl.ds(pl.multiple_of((2 * d + half) * piece + q * w, w), w)],
                tiles.at[slot, :, half * w : (half + 1) * w],
                tile_sem.at[slot, half],
            )
            for half in range(2)
        ]

    def start_fetch(q, d, slot):
        for copy in fetch(q, d, slot):
            copy.start()

    def wait_fetch(slot):
        for copy in fetch(0, 0, slot):
            copy.wait()

    start_fetch(0, order(0), 0)

    barrier = pltpu.get_barrier_semaphore()
    for mask in range(1, cols):
        pl.semaphore_signal(barrier, 1, device_id=(r, c ^ mask), device_id_type=MESH)
    pl.semaphore_signal(barrier, 1, device_id=mate, device_id_type=MESH)

    @pl.when(has_up)
    def _():
        pl.semaphore_signal(barrier, 1, device_id=upper, device_id_type=MESH)

    @pl.when(has_low)
    def _():
        pl.semaphore_signal(barrier, 1, device_id=lower, device_id_type=MESH)

    pl.semaphore_wait(barrier, cols + jnp.where(has_up, 1, 0) + jnp.where(has_low, 1, 0))

    def share(mask):
        return remote(x_ref, xs.at[c], xs_send.at[mask], xs_recv.at[mask], (r, c ^ mask))

    near = [mask for mask in range(1, cols) if mask & (mask - 1) == 0]
    far = [mask for mask in range(1, cols) if mask not in near]
    for mask in near:
        share(mask).start()
    xs[c] = x_ref[...]
    out_ref[...] = jnp.zeros_like(out_ref)
    for mask in near:
        share(mask).wait_send()
    for mask in far:
        share(mask).start()
    for mask in near + far:
        share(mask).wait_recv()

    def pair(g):
        return remote(both.at[g, 1 - core], theirs.at[g], pair_send.at[g], pair_recv.at[g], mate)

    def sum_up(q, d):
        g = q * planes + d
        slot = q * (planes + 1) + d
        return remote(both.at[g, core], sums.at[slot], sum_send.at[g], sum_recv.at[slot], upper)

    def sum_down(q, d):
        g = q * planes + d
        slot = q * (planes + 1) + jnp.where(d == z - 1, planes, d)
        return remote(both.at[g, core], sums.at[slot], sum_send.at[g], sum_recv.at[slot], lower)

    def wait_sum(slot):
        remote(sums.at[slot], sums.at[slot], sum_send.at[0], sum_recv.at[slot], upper).wait_recv()

    def chain(q, d):
        g = q * planes + d
        slot = q * (planes + 1) + d
        pair(g).wait_recv()
        incoming = jnp.where(d > z, has_low, has_up)

        @pl.when(incoming)
        def _():
            wait_sum(slot)
            both[g, core] = both[g, core] + theirs[g] + sums[slot]

        @pl.when(jnp.logical_not(incoming))
        def _():
            both[g, core] = both[g, core] + theirs[g]

        @pl.when(d > z)
        def _():
            sum_up(q, d).start()

        @pl.when(d < z)
        def _():
            sum_down(q, d).start()

    def hop_up(q, d):
        g, slot = q * planes + d, q * (planes + 1) + d
        return remote(image.at[g, core], image.at[g, core], hop_send.at[slot], hop_recv.at[g], upper)

    def hop_down(q, d):
        g, slot = q * planes + d, q * (planes + 1) + jnp.where(d == z, planes, d)
        return remote(image.at[g, core], image.at[g, core], hop_send.at[slot], hop_recv.at[g], lower)

    def to_mate(g):
        return remote(image.at[g, core], image.at[g, core], mate_send.at[g], mate_recv.at[g], mate)

    def from_mate(g):
        other = image.at[g, 1 - core]
        return remote(other, other, mate_send.at[g], mate_recv.at[g], mate)

    def finish(q):
        g = q * planes + z
        pair(g).wait_recv()
        both[g, core] = both[g, core] + theirs[g]

        @pl.when(has_low)
        def _():
            slot = q * (planes + 1) + z
            wait_sum(slot)
            both[g, core] = both[g, core] + sums[slot]

        @pl.when(has_up)
        def _():
            slot = q * (planes + 1) + planes
            wait_sum(slot)
            both[g, core] = both[g, core] + sums[slot]

        image[g, core] = both[g, core].astype(jnp.bfloat16)

        @pl.when(has_up)
        def _():
            hop_up(q, z).start()

        @pl.when(has_low)
        def _():
            hop_down(q, z).start()

        to_mate(g).start()

    def first(t, i):
        d = order(i)
        slot = lax.rem(i, 2)
        more = i < planes - 1
        again = jnp.logical_and(t < 2, t + 1 < chunks)
        next_q = jnp.where(more, t, jnp.where(again, t + 1, jnp.maximum(t - 2, 0)))
        next_d = jnp.where(more, order(jnp.minimum(i + 1, planes - 1)), jnp.where(again, order(0), z))
        start_fetch(next_q, next_d, 1 - slot)
        wait_fetch(slot)
        g = t * planes + d
        block = xs[...].reshape(cols * piece, width)
        value = lax.dot_general(tiles[slot], block, CONTRACT_ROWS, preferred_element_type=jnp.float32)
        both[g] = value.reshape(2, w, width)
        pair(g).start()

        @pl.when(i > 0)
        def _():
            chain(t, order(jnp.maximum(i - 1, 0)))

    def receive(q, i):
        d = order(planes - 1 - i)
        g = q * planes + d

        @pl.when(d != z)
        def _():
            arrived = image.at[g, core]
            remote(arrived, arrived, mate_send.at[g], hop_recv.at[g], mate).wait_recv()

            @pl.when(jnp.logical_and(d < z, has_up))
            def _():
                hop_up(q, d).start()

            @pl.when(jnp.logical_and(d > z, has_low))
            def _():
                hop_down(q, d).start()

            to_mate(g).start()

    def second(t, i):
        q = t - 2
        d = order(planes - 1 - i)
        g = q * planes + d
        slot = lax.rem(i, 2)
        more = i < planes - 1
        ahead = t + 1 < chunks
        next_q = jnp.where(more, q, jnp.where(ahead, t + 1, t - 1))
        next_d = jnp.where(more, order(jnp.maximum(planes - 2 - i, 0)), jnp.where(ahead, order(0), z))

        @pl.when(jnp.logical_or(more, t < chunks + 1))
        def _():
            start_fetch(next_q, next_d, 1 - slot)

        from_mate(g).wait_recv()
        wait_fetch(slot)
        out_ref[...] += jnp.dot(
            tiles[slot], image[g].reshape(2 * w, width), preferred_element_type=jnp.float32
        )

    @pl.loop(0, chunks + 2)
    def _(t):
        @pl.when(t < chunks)
        def _():
            @pl.loop(0, planes)
            def _(i):
                first(t, i)

        @pl.when(jnp.logical_and(t >= 1, t <= chunks))
        def _():
            finish(t - 1)

        @pl.when(t >= 2)
        def _():
            @pl.loop(0, planes + 1)
            def _(i):
                @pl.when(i < planes)
                def _():
                    receive(t - 2, i)

                @pl.when(i > 0)
                def _():
                    second(t, jnp.maximum(i - 1, 0))

    for mask in far:
        share(mask).wait_send()

    @pl.loop(0, chunks)
    def _(q):
        @pl.loop(0, planes)
        def _(d):
            g = q * planes + d
            pair(g).wait_send()
            to_mate(g).wait_send()

            @pl.when(d > z)
            def _():
                sum_up(q, d).wait_send()

            @pl.when(d < z)
            def _():
                sum_down(q, d).wait_send()

            @pl.when(jnp.logical_and(d <= z, has_up))
            def _():
                hop_up(q, d).wait_send()

            @pl.when(jnp.logical_and(d >= z, has_low))
            def _():
                hop_down(q, d).wait_send()


def two_products(gram, start_basis):
    rows, cols = lax.axis_size("row"), lax.axis_size("col")
    planes = rows // 2
    piece, width = start_basis.shape
    chunks = max(1, min(4, piece // 128))
    w = piece // chunks
    grains, slots = chunks * planes, chunks * (planes + 1)
    dma = pltpu.SemaphoreType.DMA
    return pl.pallas_call(
        functools.partial(products_kernel, rows, cols, chunks),
        out_shape=jax.ShapeDtypeStruct((gram.shape[0], width), jnp.float32),
        in_specs=[pl.BlockSpec(memory_space=pl.ANY), pl.BlockSpec(memory_space=pltpu.VMEM)],
        out_specs=pl.BlockSpec(memory_space=pltpu.VMEM),
        scratch_shapes=[
            pltpu.VMEM((2, gram.shape[0], 2 * w), jnp.bfloat16),
            dma((2, 2)),
            pltpu.VMEM((cols, piece, width), jnp.bfloat16),
            dma((cols,)),
            dma((cols,)),
            pltpu.VMEM((grains, 2, w, width), jnp.float32),
            pltpu.VMEM((grains, w, width), jnp.float32),
            dma((grains,)),
            dma((grains,)),
            pltpu.VMEM((slots, w, width), jnp.float32),
            dma((grains,)),
            dma((slots,)),
            pltpu.VMEM((grains, 2, w, width), jnp.bfloat16),
            dma((slots,)),
            dma((grains,)),
            dma((grains,)),
            dma((grains,)),
        ],
        compiler_params=pltpu.CompilerParams(
            collective_id=0, has_side_effects=True, vmem_limit_bytes=60 << 20
        ),
        name="two_products",
        cost_estimate=pl.CostEstimate(
            flops=4 * gram.size * width, bytes_accessed=4 * gram.size, transcendentals=0
        ),
    )(gram, start_basis)


def flip(value, axis, mask):
    size = lax.axis_size(axis)
    return lax.ppermute(value, axis, [(i, i ^ mask) for i in range(size)])


def gather_flips(block, axis):
    size, me = lax.axis_size(axis), lax.axis_index(axis)
    arrived = [block] + [flip(block, axis, mask) for mask in range(1, size)]
    stacked = jnp.zeros((size,) + block.shape, block.dtype)
    for mask, piece in enumerate(arrived):
        stacked = lax.dynamic_update_slice_in_dim(stacked, piece[None], me ^ mask, 0)
    return stacked.reshape((size * block.shape[0],) + block.shape[1:])


def scatter_sum_flips(parts, axis, wire):
    size, me = lax.axis_size(axis), lax.axis_index(axis)
    share = parts.shape[0] // size
    take = lambda owner: lax.dynamic_slice_in_dim(parts, owner * share, share, 0)
    total = take(me)
    for mask in range(1, size):
        total = total + flip(take(me ^ mask).astype(wire), axis, mask).astype(jnp.float32)
    return total


def sum_rows(value, beside):
    size, me = lax.axis_size("row"), lax.axis_index("row")
    core = me % 2
    half = value.shape[0] // 2
    take = lambda index: lax.dynamic_slice_in_dim(value, index * half, half, 0)
    pair = take(core) + flip(take(1 - core), "row", 1)
    arrived = [flip(pair, "row", mask) for mask in range(2, size, 2)]
    arrived, beside = lax.optimization_barrier((arrived, beside))
    total = pair
    for piece in arrived:
        total = total + piece
    back = flip(total, "row", 1)
    low = jnp.where(core == 0, total, back)
    high = jnp.where(core == 0, back, total)
    return jnp.concatenate([low, high], axis=0), beside


def dot32(a, b, dims=(((1,), (0,)), ((), ()))):
    return lax.dot_general(a, b, dims, precision=HIGHEST, preferred_element_type=jnp.float32)


ALONG = (((1,), (1,)), ((), ()))


def invert_block(work):
    n = work.shape[0]
    lane = lax.broadcasted_iota(jnp.int32, (1, n), 1)
    down = lax.broadcasted_iota(jnp.int32, (n, 1), 0)

    def step(j, pivots):
        values = work[...]
        row = work[pl.ds(j, 1), :]
        here = lane == j
        column = jnp.sum(jnp.where(here, values, 0.0), axis=1, keepdims=True)
        pivot = jnp.sum(jnp.where(here, row, 0.0), axis=1, keepdims=True)
        multiple = jnp.where(down > j, column / pivot, 0.0)
        kept = jnp.where(here & (down > j), 0.0, values)
        work[...] = kept - multiple * jnp.where(here, 1.0, row)
        return jnp.where(down == j, pivot, pivots)

    pivots = lax.fori_loop(0, n, step, jnp.ones((n, 1), jnp.float32))
    across = lax.broadcasted_iota(jnp.int32, (n, n), 1)
    unit = jnp.where(across < down, work[...], jnp.where(across == down, 1.0, 0.0))
    return unit * lax.rsqrt(pivots)


def inverse_kernel(gram_ref, out_ref, work):
    half = work.shape[0]
    work[...] = gram_ref[:half, :half]
    inv11 = invert_block(work)
    a21 = gram_ref[half:, :half]
    l21 = dot32(a21, inv11, ALONG)
    work[...] = gram_ref[half:, half:] - dot32(l21, l21, ALONG)
    inv22 = invert_block(work)
    out_ref[:half, :half] = inv11
    out_ref[:half, half:] = jnp.zeros((half, half), jnp.float32)
    out_ref[half:, :half] = -dot32(inv22, dot32(l21, inv11))
    out_ref[half:, half:] = inv22


def inverse_factor(small_gram):
    half = small_gram.shape[0] // 2
    return pl.pallas_call(
        inverse_kernel,
        out_shape=jax.ShapeDtypeStruct(small_gram.shape, jnp.float32),
        scratch_shapes=[pltpu.VMEM((half, half), jnp.float32)],
        name="inverse_factor",
    )(small_gram)


def gram_kernel(y_ref, out_ref):
    @pl.when(pl.program_id(0) == 0)
    def _():
        out_ref[...] = jnp.zeros_like(out_ref)

    y = y_ref[...]
    out_ref[...] += lax.dot_general(y, y, CONTRACT_ROWS, preferred_element_type=jnp.float32)


def block_gram(y):
    tile = math.gcd(y.shape[0], 1024)
    size = y.shape[1]
    return pl.pallas_call(
        gram_kernel,
        grid=(y.shape[0] // tile,),
        in_specs=[pl.BlockSpec((tile, size), lambda i: (i, 0))],
        out_specs=pl.BlockSpec((size, size), lambda i: (0, 0)),
        out_shape=jax.ShapeDtypeStruct((size, size), jnp.float32),
        name="block_gram",
        cost_estimate=pl.CostEstimate(
            flops=2 * y.shape[0] * size * size, bytes_accessed=2 * y.size, transcendentals=0
        ),
    )(y)


def cross_kernel(slab_ref, y_ref, out_ref):
    @pl.when(pl.program_id(0) == 0)
    def _():
        out_ref[...] = jnp.zeros_like(out_ref)

    y = y_ref[...]
    slab = slab_ref[...]
    high = slab.astype(jnp.bfloat16)
    low = (slab - high.astype(jnp.float32)).astype(jnp.bfloat16)
    term = lambda a: lax.dot_general(a, y, CONTRACT_ROWS, preferred_element_type=jnp.float32)
    out_ref[...] += term(high) + term(low)


def cross_product(slab, y):
    tile = math.gcd(y.shape[0], 512)
    wide, size = slab.shape[1], y.shape[1]
    return pl.pallas_call(
        cross_kernel,
        grid=(y.shape[0] // tile,),
        in_specs=[
            pl.BlockSpec((tile, wide), lambda i: (i, 0)),
            pl.BlockSpec((tile, size), lambda i: (i, 0)),
        ],
        out_specs=pl.BlockSpec((wide, size), lambda i: (0, 0)),
        out_shape=jax.ShapeDtypeStruct((wide, size), jnp.float32),
        name="cross_product",
        cost_estimate=pl.CostEstimate(
            flops=4 * slab.size * size, bytes_accessed=4 * slab.size, transcendentals=0
        ),
    )(slab, y)


def body(gram, start_basis, slab, order, modes):
    rows, cols = lax.axis_size("row"), lax.axis_size("col")
    partial = two_products(gram, start_basis)
    second = scatter_sum_flips(partial, "col", jnp.bfloat16)
    block_second = gather_flips(second.astype(jnp.bfloat16), "col")
    small_gram, crossed = sum_rows(block_gram(block_second), cross_product(slab, block_second))
    crossed = lax.psum_scatter(crossed, "row", scatter_dimension=0, tiled=True)
    inverse = inverse_factor(small_gram)
    proj = dot32(inverse, crossed, ALONG)
    core_out = dot32(second, inverse, ALONG) * math.sqrt(order)
    count = rows * cols
    share = proj.shape[0] // count
    moved = lax.all_to_all(
        proj.reshape(count, share, proj.shape[1]), ("row", "col"), split_axis=0, concat_axis=0, tiled=True
    )
    moved = moved.reshape(rows, cols, share, proj.shape[1]).transpose(2, 1, 0, 3)
    return core_out, moved.reshape(share * modes, -1)


NMODE = 16


def solution(mesh):
    def whole(gram, start_basis, slab):
        order = gram.shape[0]
        inner = lambda g, s, w: body(g, s, w, order, NMODE)
        in_specs = (P("row", "col"), P(("row", "col"), None), P("row", "col"))
        out_specs = (P(("row", "col"), None), P(("row", "col"), None))
        return jax.shard_map(
            inner, mesh=mesh, in_specs=in_specs, out_specs=out_specs, check_vma=False
        )(gram, start_basis, slab)

    return whole
```

```python
import functools
import math

import jax
import jax.numpy as jnp
from jax import lax
from jax.experimental import pallas as pl
from jax.experimental.pallas import tpu as pltpu
from jax.sharding import PartitionSpec as P

HIGHEST = lax.Precision.HIGHEST
CONTRACT_ROWS = (((0,), (0,)), ((), ()))
MESH = pl.DeviceIdType.MESH


def far_first(z, planes, i):
    below, above = z, planes - 1 - z
    less, more = jnp.minimum(below, above), jnp.maximum(below, above)
    lone = i < more - less
    rest = i - (more - less)
    distance = jnp.where(lone, more - i, less - lax.div(rest, 2))
    upward = jnp.where(lone, above >= below, lax.rem(rest, 2) == 0)
    return jnp.where(upward, z + distance, z - distance)


def products_kernel(
    rows, cols, chunks, gram, x_ref, out_ref,
    tiles, tile_sem, xs, xs_send, xs_recv, fwd_send, fwd_recv,
    both, theirs, pair_send, pair_recv,
    sums, sum_send, sum_recv,
    image, hop_send, hop_recv, mate_send, mate_recv,
):
    planes = rows // 2
    r, c = lax.axis_index("row"), lax.axis_index("col")
    z, core = lax.div(r, 2), lax.rem(r, 2)
    piece, width = x_ref.shape
    w = piece // chunks
    mate = (r + 1 - 2 * core, c)
    upper, lower = (jnp.minimum(r + 2, rows - 1), c), (jnp.maximum(r - 2, 0), c)
    has_up, has_low = z < planes - 1, z > 0
    order = lambda i: far_first(z, planes, i)

    def remote(src, dst, send, recv, to):
        return pltpu.make_async_remote_copy(
            src_ref=src, dst_ref=dst, send_sem=send, recv_sem=recv, device_id=to, device_id_type=MESH
        )

    def fetch(q, d, slot):
        return [
            pltpu.make_async_copy(
                gram.at[:, pl.ds(pl.multiple_of((2 * d + side) * piece + q * w, w), w)],
                tiles.at[slot, :, side * w : (side + 1) * w],
                tile_sem.at[slot, side],
            )
            for side in range(2)
        ]

    def start_fetch(q, d, slot):
        for copy in fetch(q, d, slot):
            copy.start()

    def wait_fetch(slot):
        for copy in fetch(0, 0, slot):
            copy.wait()

    start_fetch(0, order(0), 0)

    barrier = pltpu.get_barrier_semaphore()
    for mask in range(1, cols):
        pl.semaphore_signal(barrier, 1, device_id=(r, c ^ mask), device_id_type=MESH)
    pl.semaphore_signal(barrier, 1, device_id=mate, device_id_type=MESH)

    @pl.when(has_up)
    def _():
        pl.semaphore_signal(barrier, 1, device_id=upper, device_id_type=MESH)

    @pl.when(has_low)
    def _():
        pl.semaphore_signal(barrier, 1, device_id=lower, device_id_type=MESH)

    pl.semaphore_wait(barrier, cols + jnp.where(has_up, 1, 0) + jnp.where(has_low, 1, 0))

    def share(mask):
        return remote(x_ref, xs.at[c], xs_send.at[mask], xs_recv.at[mask], (r, c ^ mask))

    half = piece // 2
    relay = cols == 4
    near = [mask for mask in range(1, cols) if mask & (mask - 1) == 0]
    far = [mask for mask in range(1, cols) if mask not in near]

    def forward(mask):
        low, to = (0, 2) if mask == 1 else (half, 1)
        part = xs.at[c ^ mask, low : low + half]
        return remote(part, part, fwd_send.at[mask - 1], fwd_recv.at[mask - 1], (r, c ^ to))

    def forwarded(mask):
        low = 0 if mask == 1 else half
        part = xs.at[c ^ 3, low : low + half]
        return remote(part, part, fwd_send.at[mask - 1], fwd_recv.at[mask - 1], (r, c ^ mask))

    for mask in near:
        share(mask).start()
    xs[c] = x_ref[...]
    out_ref[...] = jnp.zeros_like(out_ref)
    if relay:
        for mask in near:
            share(mask).wait_recv()
            forward(mask).start()
        for mask in near:
            forwarded(mask).wait_recv()
    else:
        for mask in near:
            share(mask).wait_send()
        for mask in far:
            share(mask).start()
        for mask in near + far:
            share(mask).wait_recv()

    def pair(g):
        return remote(both.at[g, 1 - core], theirs.at[g], pair_send.at[g], pair_recv.at[g], mate)

    def sum_up(q, d):
        g = q * planes + d
        slot = q * (planes + 1) + d
        return remote(both.at[g, core], sums.at[slot], sum_send.at[g], sum_recv.at[slot], upper)

    def sum_down(q, d):
        g = q * planes + d
        slot = q * (planes + 1) + jnp.where(d == z - 1, planes, d)
        return remote(both.at[g, core], sums.at[slot], sum_send.at[g], sum_recv.at[slot], lower)

    def wait_sum(slot):
        remote(sums.at[slot], sums.at[slot], sum_send.at[0], sum_recv.at[slot], upper).wait_recv()

    def chain(q, d):
        g = q * planes + d
        slot = q * (planes + 1) + d
        pair(g).wait_recv()
        extra = incoming(d)

        @pl.when(extra)
        def _():
            wait_sum(slot)
            both[g, core] = both[g, core] + theirs[g] + sums[slot]

        @pl.when(jnp.logical_not(extra))
        def _():
            both[g, core] = both[g, core] + theirs[g]

        @pl.when(d > z)
        def _():
            sum_up(q, d).start()

        @pl.when(d < z)
        def _():
            sum_down(q, d).start()

    def hop_up(q, d):
        g, slot = q * planes + d, q * (planes + 1) + d
        return remote(image.at[g, core], image.at[g, core], hop_send.at[slot], hop_recv.at[g], upper)

    def hop_down(q, d):
        g, slot = q * planes + d, q * (planes + 1) + jnp.where(d == z, planes, d)
        return remote(image.at[g, core], image.at[g, core], hop_send.at[slot], hop_recv.at[g], lower)

    def to_mate(g):
        return remote(image.at[g, core], image.at[g, core], mate_send.at[g], mate_recv.at[g], mate)

    def from_mate(g):
        other = image.at[g, 1 - core]
        return remote(other, other, mate_send.at[g], mate_recv.at[g], mate)

    def finish(q):
        g = q * planes + z
        pair(g).wait_recv()
        both[g, core] = both[g, core] + theirs[g]

        @pl.when(has_low)
        def _():
            slot = q * (planes + 1) + z
            wait_sum(slot)
            both[g, core] = both[g, core] + sums[slot]

        @pl.when(has_up)
        def _():
            slot = q * (planes + 1) + planes
            wait_sum(slot)
            both[g, core] = both[g, core] + sums[slot]

        image[g, core] = both[g, core].astype(jnp.bfloat16)

        @pl.when(has_up)
        def _():
            hop_up(q, z).start()

        @pl.when(has_low)
        def _():
            hop_down(q, z).start()

        to_mate(g).start()

    def incoming(d):
        return jnp.where(d > z, has_low, has_up)

    def begin(s):
        early = s < chunks
        start_fetch(jnp.where(early, s, s - 2), jnp.where(early, order(0), z), 0)

    def first(s, i):
        d = order(i)
        mixed = s >= 2
        slot = jnp.where(mixed, jnp.minimum(i, 1), lax.rem(i, 2))
        more = jnp.where(mixed, i == 0, i < planes - 1)

        @pl.when(more)
        def _():
            start_fetch(s, order(jnp.minimum(i + 1, planes - 1)), 1 - slot)

        @pl.when(jnp.logical_and(mixed, i > 0))
        def _():
            start_fetch(jnp.maximum(s - 2, 0), order(jnp.minimum(planes - i, planes - 1)), 0)

        @pl.when(jnp.logical_and(jnp.logical_not(mixed), i == planes - 1))
        def _():
            begin(s + 1)

        wait_fetch(slot)
        g = s * planes + d
        block = xs[...].reshape(cols * piece, width)
        value = lax.dot_general(tiles[slot], block, CONTRACT_ROWS, preferred_element_type=jnp.float32)
        both[g] = value.reshape(2, w, width)
        pair(g).start()
        before = order(jnp.maximum(i - 1, 0))

        @pl.when(jnp.logical_and(i > 0, jnp.logical_not(incoming(before))))
        def _():
            chain(s, before)

    def receive(q, i):
        d = order(planes - 1 - i)
        g = q * planes + d

        @pl.when(d != z)
        def _():
            arrived = image.at[g, core]
            remote(arrived, arrived, mate_send.at[g], hop_recv.at[g], mate).wait_recv()

            @pl.when(jnp.logical_and(d < z, has_up))
            def _():
                hop_up(q, d).start()

            @pl.when(jnp.logical_and(d > z, has_low))
            def _():
                hop_down(q, d).start()

            to_mate(g).start()

    def second(s, j):
        q = s - 2
        d = order(planes - 1 - j)
        g = q * planes + d
        mixed = s < chunks
        last = j == planes - 1
        slot = jnp.where(mixed, jnp.where(last, 1, 0), lax.rem(j, 2))

        @pl.when(jnp.logical_and(mixed, j < planes - 2))
        def _():
            start_fetch(s, order(jnp.minimum(j + 2, planes - 1)), 1)

        @pl.when(jnp.where(mixed, j == planes - 2, jnp.logical_not(last)))
        def _():
            start_fetch(q, order(jnp.maximum(planes - 2 - j, 0)), 1 - slot)

        @pl.when(jnp.logical_and(last, s < chunks + 1))
        def _():
            begin(s + 1)

        from_mate(g).wait_recv()
        wait_fetch(slot)
        out_ref[...] += jnp.dot(
            tiles[slot], image[g].reshape(2 * w, width), preferred_element_type=jnp.float32
        )

    @pl.loop(0, chunks + 2)
    def _(s):
        @pl.loop(0, planes + 1)
        def _(i):
            inside = i < planes
            here = jnp.minimum(i, planes - 1)
            linking = jnp.logical_and(inside, jnp.logical_and(s >= 1, s <= chunks))
            target = order(here)
            q = jnp.maximum(s - 1, 0)

            @pl.when(jnp.logical_and(linking, jnp.logical_and(target != z, incoming(target))))
            def _():
                chain(q, target)

            @pl.when(jnp.logical_and(linking, target == z))
            def _():
                finish(q)

            @pl.when(jnp.logical_and(inside, s < chunks))
            def _():
                first(s, here)

            @pl.when(jnp.logical_and(inside, s >= 2))
            def _():
                receive(s - 2, here)

            @pl.when(jnp.logical_and(i > 0, s >= 2))
            def _():
                second(s, jnp.maximum(i - 1, 0))

    if relay:
        for mask in near:
            share(mask).wait_send()
            forward(mask).wait_send()
    else:
        for mask in far:
            share(mask).wait_send()

    @pl.loop(0, chunks)
    def _(q):
        @pl.loop(0, planes)
        def _(d):
            g = q * planes + d
            pair(g).wait_send()
            to_mate(g).wait_send()

            @pl.when(d > z)
            def _():
                sum_up(q, d).wait_send()

            @pl.when(d < z)
            def _():
                sum_down(q, d).wait_send()

            @pl.when(jnp.logical_and(d <= z, has_up))
            def _():
                hop_up(q, d).wait_send()

            @pl.when(jnp.logical_and(d >= z, has_low))
            def _():
                hop_down(q, d).wait_send()


def two_products(gram, start_basis):
    rows, cols = lax.axis_size("row"), lax.axis_size("col")
    planes = rows // 2
    piece, width = start_basis.shape
    chunks = max(2, min(4, piece // 128))
    w = piece // chunks
    grains, slots = chunks * planes, chunks * (planes + 1)
    dma = pltpu.SemaphoreType.DMA
    return pl.pallas_call(
        functools.partial(products_kernel, rows, cols, chunks),
        out_shape=jax.ShapeDtypeStruct((gram.shape[0], width), jnp.float32),
        in_specs=[pl.BlockSpec(memory_space=pl.ANY), pl.BlockSpec(memory_space=pltpu.VMEM)],
        out_specs=pl.BlockSpec(memory_space=pltpu.VMEM),
        scratch_shapes=[
            pltpu.VMEM((2, gram.shape[0], 2 * w), jnp.bfloat16),
            dma((2, 2)),
            pltpu.VMEM((cols, piece, width), jnp.bfloat16),
            dma((cols,)),
            dma((cols,)),
            dma((2,)),
            dma((2,)),
            pltpu.VMEM((grains, 2, w, width), jnp.float32),
            pltpu.VMEM((grains, w, width), jnp.float32),
            dma((grains,)),
            dma((grains,)),
            pltpu.VMEM((slots, w, width), jnp.float32),
            dma((grains,)),
            dma((slots,)),
            pltpu.VMEM((grains, 2, w, width), jnp.bfloat16),
            dma((slots,)),
            dma((grains,)),
            dma((grains,)),
            dma((grains,)),
        ],
        compiler_params=pltpu.CompilerParams(
            collective_id=0, has_side_effects=True, vmem_limit_bytes=60 << 20
        ),
        name="two_products",
        cost_estimate=pl.CostEstimate(
            flops=4 * gram.size * width, bytes_accessed=4 * gram.size, transcendentals=0
        ),
    )(gram, start_basis)


def flip(value, axis, mask):
    size = lax.axis_size(axis)
    return lax.ppermute(value, axis, [(i, i ^ mask) for i in range(size)])


def gather_flips(block, axis):
    size, me = lax.axis_size(axis), lax.axis_index(axis)
    arrived = [block] + [flip(block, axis, mask) for mask in range(1, size)]
    stacked = jnp.zeros((size,) + block.shape, block.dtype)
    for mask, piece in enumerate(arrived):
        stacked = lax.dynamic_update_slice_in_dim(stacked, piece[None], me ^ mask, 0)
    return stacked.reshape((size * block.shape[0],) + block.shape[1:])


def scatter_sum_flips(parts, axis, wire):
    size, me = lax.axis_size(axis), lax.axis_index(axis)
    share = parts.shape[0] // size
    take = lambda owner: lax.dynamic_slice_in_dim(parts, owner * share, share, 0)
    total = take(me)
    for mask in range(1, size):
        total = total + flip(take(me ^ mask).astype(wire), axis, mask).astype(jnp.float32)
    return total


def sum_rows(value, beside):
    size, me = lax.axis_size("row"), lax.axis_index("row")
    core = me % 2
    half = value.shape[0] // 2
    take = lambda index: lax.dynamic_slice_in_dim(value, index * half, half, 0)
    pair = take(core) + flip(take(1 - core), "row", 1)
    arrived = [flip(pair, "row", mask) for mask in range(2, size, 2)]
    arrived, beside = lax.optimization_barrier((arrived, beside))
    total = pair
    for piece in arrived:
        total = total + piece
    back = flip(total, "row", 1)
    low = jnp.where(core == 0, total, back)
    high = jnp.where(core == 0, back, total)
    return jnp.concatenate([low, high], axis=0), beside


def dot32(a, b, dims=(((1,), (0,)), ((), ()))):
    return lax.dot_general(a, b, dims, precision=HIGHEST, preferred_element_type=jnp.float32)


ALONG = (((1,), (1,)), ((), ()))


BATCH = 8


def pick(value, j):
    return jnp.take_along_axis(value, jnp.full(value.shape, j, jnp.int32), axis=1)


def invert_block(work):
    n = work.shape[0]
    lane = lax.broadcasted_iota(jnp.int32, (BATCH, n), 1)
    down = lax.broadcasted_iota(jnp.int32, (n, n), 0)
    across = lax.broadcasted_iota(jnp.int32, (n, n), 1)
    level = lax.broadcasted_iota(jnp.int32, (BATCH, n), 0)

    def step(b, pivots):
        j = b * BATCH
        panel = work[pl.ds(pl.multiple_of(j, BATCH), BATCH), :]
        rows = [jnp.broadcast_to(panel[t : t + 1], (BATCH, n)) for t in range(BATCH)]
        entries = [[pick(rows[t], j + s) for s in range(t, BATCH)] for t in range(BATCH)]
        left = jnp.zeros((BATCH, n), jnp.float32)
        right = jnp.zeros((BATCH, n), jnp.float32)
        for t in range(BATCH):
            here = lane == j + t
            inverse = 1.0 / entries[t][0]
            pivots = jnp.where(here, entries[t][0], pivots)
            clean = jnp.where(here, 1.0, rows[t])
            for s in range(t + 1, BATCH):
                factor = entries[t][s - t] * inverse
                rows[s] = jnp.where(here, 0.0, rows[s]) - factor * clean
                for u in range(s, BATCH):
                    entries[s][u - s] = entries[s][u - s] - factor * entries[t][u - t]
            later = (lane > j + t) & (lane < j + BATCH)
            left = jnp.where(level == t, jnp.where(lane > j + t, rows[t] * inverse, 0.0), left)
            right = jnp.where(level == t, jnp.where(later, 0.0, clean), right)
        update = dot32(left, right, CONTRACT_ROWS)
        fresh = (across >= j) & (across < j + BATCH) & (down > across)
        work[...] = jnp.where(fresh, 0.0, work[...]) - update
        return pivots

    pivots = lax.fori_loop(0, n // BATCH, step, jnp.ones((BATCH, n), jnp.float32))
    unit = jnp.where(across < down, work[...], jnp.where(across == down, 1.0, 0.0))
    scale = jnp.sum(jnp.where(across == down, lax.rsqrt(pivots[:1]), 0.0), axis=1, keepdims=True)
    return unit * scale


def inverse_kernel(gram_ref, out_ref, work):
    half = work.shape[0]
    work[...] = gram_ref[:half, :half]
    inv11 = invert_block(work)
    a21 = gram_ref[half:, :half]
    l21 = dot32(a21, inv11, ALONG)
    work[...] = gram_ref[half:, half:] - dot32(l21, l21, ALONG)
    inv22 = invert_block(work)
    out_ref[:half, :half] = inv11
    out_ref[:half, half:] = jnp.zeros((half, half), jnp.float32)
    out_ref[half:, :half] = -dot32(inv22, dot32(l21, inv11))
    out_ref[half:, half:] = inv22


def inverse_factor(small_gram):
    half = small_gram.shape[0] // 2
    return pl.pallas_call(
        inverse_kernel,
        out_shape=jax.ShapeDtypeStruct(small_gram.shape, jnp.float32),
        scratch_shapes=[pltpu.VMEM((half, half), jnp.float32)],
        name="inverse_factor",
    )(small_gram)


def gram_kernel(y_ref, out_ref):
    @pl.when(pl.program_id(0) == 0)
    def _():
        out_ref[...] = jnp.zeros_like(out_ref)

    y = y_ref[...]
    out_ref[...] += lax.dot_general(y, y, CONTRACT_ROWS, preferred_element_type=jnp.float32)


def block_gram(y):
    tile = math.gcd(y.shape[0], 1024)
    size = y.shape[1]
    return pl.pallas_call(
        gram_kernel,
        grid=(y.shape[0] // tile,),
        in_specs=[pl.BlockSpec((tile, size), lambda i: (i, 0))],
        out_specs=pl.BlockSpec((size, size), lambda i: (0, 0)),
        out_shape=jax.ShapeDtypeStruct((size, size), jnp.float32),
        name="block_gram",
        cost_estimate=pl.CostEstimate(
            flops=2 * y.shape[0] * size * size, bytes_accessed=2 * y.size, transcendentals=0
        ),
    )(y)


def cross_kernel(slab_ref, y_ref, out_ref):
    @pl.when(pl.program_id(0) == 0)
    def _():
        out_ref[...] = jnp.zeros_like(out_ref)

    y = y_ref[...]
    slab = slab_ref[...]
    high = slab.astype(jnp.bfloat16)
    low = (slab - high.astype(jnp.float32)).astype(jnp.bfloat16)
    term = lambda a: lax.dot_general(a, y, CONTRACT_ROWS, preferred_element_type=jnp.float32)
    out_ref[...] += term(high) + term(low)


def cross_product(slab, y):
    tile = math.gcd(y.shape[0], 512)
    wide, size = slab.shape[1], y.shape[1]
    return pl.pallas_call(
        cross_kernel,
        grid=(y.shape[0] // tile,),
        in_specs=[
            pl.BlockSpec((tile, wide), lambda i: (i, 0)),
            pl.BlockSpec((tile, size), lambda i: (i, 0)),
        ],
        out_specs=pl.BlockSpec((wide, size), lambda i: (0, 0)),
        out_shape=jax.ShapeDtypeStruct((wide, size), jnp.float32),
        name="cross_product",
        cost_estimate=pl.CostEstimate(
            flops=4 * slab.size * size, bytes_accessed=4 * slab.size, transcendentals=0
        ),
    )(slab, y)


def shares_kernel(
    partial, slab, second_ref, gram_ref, crossed_ref,
    out1, in1, out2, in2, send1, recv1, send2, recv2,
    ys, y_send, y_recv, fwd_send, fwd_recv, tiles, tile_sem,
):
    r, c = lax.axis_index("row"), lax.axis_index("col")
    piece = second_ref.shape[0]
    half = piece // 2
    steps = 8
    part = piece * 4 // steps
    routes = ((1, 2), (2, 1))
    place = [c, c ^ 1, c ^ 2, c ^ 3]

    def remote(src, dst, send, recv, mask):
        return pltpu.make_async_remote_copy(
            src_ref=src, dst_ref=dst, send_sem=send, recv_sem=recv, device_id=(r, c ^ mask), device_id_type=MESH
        )

    def fetch(step):
        start = place[step // 2] * piece + (step % 2) * part
        return pltpu.make_async_copy(
            slab.at[pl.ds(pl.multiple_of(start, part), part), :], tiles.at[step % 2], tile_sem.at[step % 2]
        )

    fetch(0).start()
    fetch(1).start()
    barrier = pltpu.get_barrier_semaphore()
    for mask in (1, 2):
        pl.semaphore_signal(barrier, 1, device_id=(r, c ^ mask), device_id_type=MESH)
    pl.semaphore_wait(barrier, 2)

    def rows_of(owner, route):
        return partial[pl.ds(pl.multiple_of(owner * piece + route * half, half), half), :]

    def leg1(route, j):
        mask = routes[route][0]
        return remote(out1.at[route, j], in1.at[route, j], send1.at[route, j], recv1.at[route, j], mask)

    def leg2(route):
        mask = routes[route][1]
        return remote(out2.at[route], in2.at[route], send2.at[route], recv2.at[route], mask)

    for j in range(2):
        for route in range(2):
            owner = place[3] if j == 0 else place[routes[route][0]]
            out1[route, j] = rows_of(owner, route).astype(jnp.bfloat16)
            leg1(route, j).start()
    for route in range(2):
        leg1(route, 0).wait_recv()
        total = rows_of(place[routes[route][1]], route) + in1[route, 0].astype(jnp.float32)
        out2[route] = total.astype(jnp.bfloat16)
        leg2(route).start()
    for route in range(2):
        leg1(route, 1).wait_recv()
        leg2(route).wait_recv()
        total = rows_of(c, route) + in1[route, 1].astype(jnp.float32) + in2[route].astype(jnp.float32)
        second_ref[route * half : (route + 1) * half, :] = total
        ys[c, route * half : (route + 1) * half, :] = total.astype(jnp.bfloat16)

    def share(mask):
        return remote(ys.at[c], ys.at[c], y_send.at[mask - 1], y_recv.at[mask - 1], mask)

    def shared(mask):
        block = ys.at[c ^ mask]
        return remote(block, block, y_send.at[mask - 1], y_recv.at[mask - 1], mask)

    def forward(mask):
        low, to = (0, 2) if mask == 1 else (half, 1)
        block = ys.at[c ^ mask, low : low + half]
        return remote(block, block, fwd_send.at[mask - 1], fwd_recv.at[mask - 1], to)

    def forwarded(mask):
        low = 0 if mask == 1 else half
        block = ys.at[c ^ 3, low : low + half]
        return remote(block, block, fwd_send.at[mask - 1], fwd_recv.at[mask - 1], mask)

    def multiply(m):
        y = ys[place[m]]
        term = lax.dot_general(y, y, CONTRACT_ROWS, preferred_element_type=jnp.float32)
        gram_ref[...] = term if m == 0 else gram_ref[...] + term
        for step in (2 * m, 2 * m + 1):
            fetch(step).wait()
            tile = tiles[step % 2]
            high = tile.astype(jnp.bfloat16)
            low = (tile - high.astype(jnp.float32)).astype(jnp.bfloat16)
            rows = ys[place[m], (step % 2) * part : (step % 2 + 1) * part, :]
            dot = lambda a: lax.dot_general(a, rows, CONTRACT_ROWS, preferred_element_type=jnp.float32)
            value = dot(high) + dot(low)
            crossed_ref[...] = value if step == 0 else crossed_ref[...] + value
            if step + 2 < steps:
                fetch(step + 2).start()

    for mask in (1, 2):
        share(mask).start()
    multiply(0)
    for mask in (1, 2):
        shared(mask).wait_recv()
        forward(mask).start()
    multiply(1)
    multiply(2)
    for mask in (1, 2):
        forwarded(mask).wait_recv()
    multiply(3)
    for mask in (1, 2):
        share(mask).wait_send()
        forward(mask).wait_send()
    for route in range(2):
        leg1(route, 0).wait_send()
        leg1(route, 1).wait_send()
        leg2(route).wait_send()


def share_and_multiply(partial, slab):
    piece, width = partial.shape[0] // 4, partial.shape[1]
    half = piece // 2
    wide = slab.shape[1]
    dma = pltpu.SemaphoreType.DMA
    vmem = pl.BlockSpec(memory_space=pltpu.VMEM)
    return pl.pallas_call(
        shares_kernel,
        out_shape=(
            jax.ShapeDtypeStruct((piece, width), jnp.float32),
            jax.ShapeDtypeStruct((width, width), jnp.float32),
            jax.ShapeDtypeStruct((wide, width), jnp.float32),
        ),
        in_specs=[vmem, pl.BlockSpec(memory_space=pl.ANY)],
        out_specs=(vmem, vmem, vmem),
        scratch_shapes=[
            pltpu.VMEM((2, 2, half, width), jnp.bfloat16),
            pltpu.VMEM((2, 2, half, width), jnp.bfloat16),
            pltpu.VMEM((2, half, width), jnp.bfloat16),
            pltpu.VMEM((2, half, width), jnp.bfloat16),
            dma((2, 2)),
            dma((2, 2)),
            dma((2,)),
            dma((2,)),
            pltpu.VMEM((4, piece, width), jnp.bfloat16),
            dma((2,)),
            dma((2,)),
            dma((2,)),
            dma((2,)),
            pltpu.VMEM((2, half, wide), jnp.float32),
            dma((2,)),
        ],
        compiler_params=pltpu.CompilerParams(
            collective_id=1, has_side_effects=True, vmem_limit_bytes=48 << 20
        ),
        name="share_and_multiply",
        cost_estimate=pl.CostEstimate(
            flops=4 * slab.size * width, bytes_accessed=4 * slab.size, transcendentals=0
        ),
    )(partial, slab)


def body(gram, start_basis, slab, order, modes):
    rows, cols = lax.axis_size("row"), lax.axis_size("col")
    partial = two_products(gram, start_basis)
    if cols == 4:
        second, grams, crossed = share_and_multiply(partial, slab)
        small_gram, _ = sum_rows(grams, grams)
    else:
        second = scatter_sum_flips(partial, "col", jnp.bfloat16)
        block_second = gather_flips(second.astype(jnp.bfloat16), "col")
        small_gram, crossed = sum_rows(block_gram(block_second), cross_product(slab, block_second))
    crossed = lax.psum_scatter(crossed, "row", scatter_dimension=0, tiled=True)
    inverse = inverse_factor(small_gram)
    proj = dot32(inverse, crossed, ALONG)
    core_out = dot32(second, inverse, ALONG) * math.sqrt(order)
    count = rows * cols
    share = proj.shape[0] // count
    moved = lax.all_to_all(
        proj.reshape(count, share, proj.shape[1]), ("row", "col"), split_axis=0, concat_axis=0, tiled=True
    )
    moved = moved.reshape(rows, cols, share, proj.shape[1]).transpose(2, 1, 0, 3)
    return core_out, moved.reshape(share * modes, -1)


NMODE = 16


def solution(mesh):
    def whole(gram, start_basis, slab):
        order = gram.shape[0]
        inner = lambda g, s, w: body(g, s, w, order, NMODE)
        in_specs = (P("row", "col"), P(("row", "col"), None), P("row", "col"))
        out_specs = (P(("row", "col"), None), P(("row", "col"), None))
        return jax.shard_map(
            inner, mesh=mesh, in_specs=in_specs, out_specs=out_specs, check_vma=False
        )(gram, start_basis, slab)

    return whole
```

```python
import functools
import math

import jax
import jax.numpy as jnp
from jax import lax
from jax.experimental import pallas as pl
from jax.experimental.pallas import tpu as pltpu
from jax.sharding import PartitionSpec as P

HIGHEST = lax.Precision.HIGHEST
CONTRACT_ROWS = (((0,), (0,)), ((), ()))
MESH = pl.DeviceIdType.MESH


def far_first(z, planes, i):
    below, above = z, planes - 1 - z
    less, more = jnp.minimum(below, above), jnp.maximum(below, above)
    lone = i < more - less
    rest = i - (more - less)
    distance = jnp.where(lone, more - i, less - lax.div(rest, 2))
    upward = jnp.where(lone, above >= below, lax.rem(rest, 2) == 0)
    return jnp.where(upward, z + distance, z - distance)


def products_kernel(
    rows, cols, chunks, gram, x_ref, out_ref,
    tiles, tile_sem, xs, xs_send, xs_recv, fwd_send, fwd_recv,
    both, theirs, pair_send, pair_recv,
    sums, sum_send, sum_recv,
    image, hop_send, hop_recv, mate_send, mate_recv,
):
    planes = rows // 2
    r, c = lax.axis_index("row"), lax.axis_index("col")
    z, core = lax.div(r, 2), lax.rem(r, 2)
    piece, width = x_ref.shape
    w = piece // chunks
    mate = (r + 1 - 2 * core, c)
    upper, lower = (jnp.minimum(r + 2, rows - 1), c), (jnp.maximum(r - 2, 0), c)
    has_up, has_low = z < planes - 1, z > 0
    order = lambda i: far_first(z, planes, i)

    def remote(src, dst, send, recv, to):
        return pltpu.make_async_remote_copy(
            src_ref=src, dst_ref=dst, send_sem=send, recv_sem=recv, device_id=to, device_id_type=MESH
        )

    def fetch(q, d, slot):
        return [
            pltpu.make_async_copy(
                gram.at[:, pl.ds(pl.multiple_of((2 * d + side) * piece + q * w, w), w)],
                tiles.at[slot, :, side * w : (side + 1) * w],
                tile_sem.at[slot, side],
            )
            for side in range(2)
        ]

    def start_fetch(q, d, slot):
        for copy in fetch(q, d, slot):
            copy.start()

    def wait_fetch(slot):
        for copy in fetch(0, 0, slot):
            copy.wait()

    start_fetch(0, order(0), 0)

    barrier = pltpu.get_barrier_semaphore()
    for mask in range(1, cols):
        pl.semaphore_signal(barrier, 1, device_id=(r, c ^ mask), device_id_type=MESH)
    pl.semaphore_signal(barrier, 1, device_id=mate, device_id_type=MESH)

    @pl.when(has_up)
    def _():
        pl.semaphore_signal(barrier, 1, device_id=upper, device_id_type=MESH)

    @pl.when(has_low)
    def _():
        pl.semaphore_signal(barrier, 1, device_id=lower, device_id_type=MESH)

    pl.semaphore_wait(barrier, cols + jnp.where(has_up, 1, 0) + jnp.where(has_low, 1, 0))

    def share(mask):
        return remote(x_ref, xs.at[c], xs_send.at[mask], xs_recv.at[mask], (r, c ^ mask))

    half = piece // 2
    relay = cols == 4
    near = [mask for mask in range(1, cols) if mask & (mask - 1) == 0]
    far = [mask for mask in range(1, cols) if mask not in near]

    def forward(mask):
        low, to = (0, 2) if mask == 1 else (half, 1)
        part = xs.at[c ^ mask, low : low + half]
        return remote(part, part, fwd_send.at[mask - 1], fwd_recv.at[mask - 1], (r, c ^ to))

    def forwarded(mask):
        low = 0 if mask == 1 else half
        part = xs.at[c ^ 3, low : low + half]
        return remote(part, part, fwd_send.at[mask - 1], fwd_recv.at[mask - 1], (r, c ^ mask))

    for mask in near:
        share(mask).start()
    xs[c] = x_ref[...]
    out_ref[...] = jnp.zeros_like(out_ref)
    if relay:
        for mask in near:
            share(mask).wait_recv()
            forward(mask).start()
        for mask in near:
            forwarded(mask).wait_recv()
    else:
        for mask in near:
            share(mask).wait_send()
        for mask in far:
            share(mask).start()
        for mask in near + far:
            share(mask).wait_recv()

    def pair(g):
        return remote(both.at[g, 1 - core], theirs.at[g], pair_send.at[g], pair_recv.at[g], mate)

    def sum_up(q, d):
        g = q * planes + d
        slot = q * (planes + 1) + d
        return remote(both.at[g, core], sums.at[slot], sum_send.at[g], sum_recv.at[slot], upper)

    def sum_down(q, d):
        g = q * planes + d
        slot = q * (planes + 1) + jnp.where(d == z - 1, planes, d)
        return remote(both.at[g, core], sums.at[slot], sum_send.at[g], sum_recv.at[slot], lower)

    def wait_sum(slot):
        remote(sums.at[slot], sums.at[slot], sum_send.at[0], sum_recv.at[slot], upper).wait_recv()

    def chain(q, d):
        g = q * planes + d
        slot = q * (planes + 1) + d
        pair(g).wait_recv()
        extra = incoming(d)

        @pl.when(extra)
        def _():
            wait_sum(slot)
            both[g, core] = both[g, core] + theirs[g] + sums[slot]

        @pl.when(jnp.logical_not(extra))
        def _():
            both[g, core] = both[g, core] + theirs[g]

        @pl.when(d > z)
        def _():
            sum_up(q, d).start()

        @pl.when(d < z)
        def _():
            sum_down(q, d).start()

    def hop_up(q, d):
        g, slot = q * planes + d, q * (planes + 1) + d
        return remote(image.at[g, core], image.at[g, core], hop_send.at[slot], hop_recv.at[g], upper)

    def hop_down(q, d):
        g, slot = q * planes + d, q * (planes + 1) + jnp.where(d == z, planes, d)
        return remote(image.at[g, core], image.at[g, core], hop_send.at[slot], hop_recv.at[g], lower)

    def to_mate(g):
        return remote(image.at[g, core], image.at[g, core], mate_send.at[g], mate_recv.at[g], mate)

    def from_mate(g):
        other = image.at[g, 1 - core]
        return remote(other, other, mate_send.at[g], mate_recv.at[g], mate)

    def finish(q):
        g = q * planes + z
        pair(g).wait_recv()
        both[g, core] = both[g, core] + theirs[g]

        @pl.when(has_low)
        def _():
            slot = q * (planes + 1) + z
            wait_sum(slot)
            both[g, core] = both[g, core] + sums[slot]

        @pl.when(has_up)
        def _():
            slot = q * (planes + 1) + planes
            wait_sum(slot)
            both[g, core] = both[g, core] + sums[slot]

        image[g, core] = both[g, core].astype(jnp.bfloat16)

        @pl.when(has_up)
        def _():
            hop_up(q, z).start()

        @pl.when(has_low)
        def _():
            hop_down(q, z).start()

        to_mate(g).start()

    def incoming(d):
        return jnp.where(d > z, has_low, has_up)

    def begin(s):
        early = s < chunks
        start_fetch(jnp.where(early, s, s - 2), jnp.where(early, order(0), z), 0)

    def first(s, i):
        d = order(i)
        mixed = s >= 2
        slot = jnp.where(mixed, jnp.minimum(i, 1), lax.rem(i, 2))
        more = jnp.where(mixed, i == 0, i < planes - 1)

        @pl.when(more)
        def _():
            start_fetch(s, order(jnp.minimum(i + 1, planes - 1)), 1 - slot)

        @pl.when(jnp.logical_and(mixed, i > 0))
        def _():
            start_fetch(jnp.maximum(s - 2, 0), order(jnp.minimum(planes - i, planes - 1)), 0)

        @pl.when(jnp.logical_and(jnp.logical_not(mixed), i == planes - 1))
        def _():
            begin(s + 1)

        wait_fetch(slot)
        g = s * planes + d
        block = xs[...].reshape(cols * piece, width)
        value = lax.dot_general(tiles[slot], block, CONTRACT_ROWS, preferred_element_type=jnp.float32)
        both[g] = value.reshape(2, w, width)
        pair(g).start()
        before = order(jnp.maximum(i - 1, 0))

        @pl.when(jnp.logical_and(i > 0, jnp.logical_not(incoming(before))))
        def _():
            chain(s, before)

    def receive(q, i):
        d = order(planes - 1 - i)
        g = q * planes + d

        @pl.when(d != z)
        def _():
            arrived = image.at[g, core]
            remote(arrived, arrived, mate_send.at[g], hop_recv.at[g], mate).wait_recv()

            @pl.when(jnp.logical_and(d < z, has_up))
            def _():
                hop_up(q, d).start()

            @pl.when(jnp.logical_and(d > z, has_low))
            def _():
                hop_down(q, d).start()

            to_mate(g).start()

    def second(s, j):
        q = s - 2
        d = order(planes - 1 - j)
        g = q * planes + d
        mixed = s < chunks
        last = j == planes - 1
        slot = jnp.where(mixed, jnp.where(last, 1, 0), lax.rem(j, 2))

        @pl.when(jnp.logical_and(mixed, j < planes - 2))
        def _():
            start_fetch(s, order(jnp.minimum(j + 2, planes - 1)), 1)

        @pl.when(jnp.where(mixed, j == planes - 2, jnp.logical_not(last)))
        def _():
            start_fetch(q, order(jnp.maximum(planes - 2 - j, 0)), 1 - slot)

        @pl.when(jnp.logical_and(last, s < chunks + 1))
        def _():
            begin(s + 1)

        from_mate(g).wait_recv()
        wait_fetch(slot)
        out_ref[...] += jnp.dot(
            tiles[slot], image[g].reshape(2 * w, width), preferred_element_type=jnp.float32
        )

    @pl.loop(0, chunks + 2)
    def _(s):
        @pl.loop(0, planes + 1)
        def _(i):
            inside = i < planes
            here = jnp.minimum(i, planes - 1)
            linking = jnp.logical_and(inside, jnp.logical_and(s >= 1, s <= chunks))
            target = order(here)
            q = jnp.maximum(s - 1, 0)

            @pl.when(jnp.logical_and(linking, jnp.logical_and(target != z, incoming(target))))
            def _():
                chain(q, target)

            @pl.when(jnp.logical_and(linking, target == z))
            def _():
                finish(q)

            @pl.when(jnp.logical_and(inside, s < chunks))
            def _():
                first(s, here)

            @pl.when(jnp.logical_and(inside, s >= 2))
            def _():
                receive(s - 2, here)

            @pl.when(jnp.logical_and(i > 0, s >= 2))
            def _():
                second(s, jnp.maximum(i - 1, 0))

    if relay:
        for mask in near:
            share(mask).wait_send()
            forward(mask).wait_send()
    else:
        for mask in far:
            share(mask).wait_send()

    @pl.loop(0, chunks)
    def _(q):
        @pl.loop(0, planes)
        def _(d):
            g = q * planes + d
            pair(g).wait_send()
            to_mate(g).wait_send()

            @pl.when(d > z)
            def _():
                sum_up(q, d).wait_send()

            @pl.when(d < z)
            def _():
                sum_down(q, d).wait_send()

            @pl.when(jnp.logical_and(d <= z, has_up))
            def _():
                hop_up(q, d).wait_send()

            @pl.when(jnp.logical_and(d >= z, has_low))
            def _():
                hop_down(q, d).wait_send()


def two_products(gram, start_basis):
    rows, cols = lax.axis_size("row"), lax.axis_size("col")
    planes = rows // 2
    piece, width = start_basis.shape
    chunks = max(2, min(4, piece // 128))
    w = piece // chunks
    grains, slots = chunks * planes, chunks * (planes + 1)
    dma = pltpu.SemaphoreType.DMA
    return pl.pallas_call(
        functools.partial(products_kernel, rows, cols, chunks),
        out_shape=jax.ShapeDtypeStruct((gram.shape[0], width), jnp.float32),
        in_specs=[pl.BlockSpec(memory_space=pl.ANY), pl.BlockSpec(memory_space=pltpu.VMEM)],
        out_specs=pl.BlockSpec(memory_space=pltpu.VMEM),
        scratch_shapes=[
            pltpu.VMEM((2, gram.shape[0], 2 * w), jnp.bfloat16),
            dma((2, 2)),
            pltpu.VMEM((cols, piece, width), jnp.bfloat16),
            dma((cols,)),
            dma((cols,)),
            dma((2,)),
            dma((2,)),
            pltpu.VMEM((grains, 2, w, width), jnp.float32),
            pltpu.VMEM((grains, w, width), jnp.float32),
            dma((grains,)),
            dma((grains,)),
            pltpu.VMEM((slots, w, width), jnp.float32),
            dma((grains,)),
            dma((slots,)),
            pltpu.VMEM((grains, 2, w, width), jnp.bfloat16),
            dma((slots,)),
            dma((grains,)),
            dma((grains,)),
            dma((grains,)),
        ],
        compiler_params=pltpu.CompilerParams(
            collective_id=0, has_side_effects=True, vmem_limit_bytes=60 << 20
        ),
        name="two_products",
        cost_estimate=pl.CostEstimate(
            flops=4 * gram.size * width, bytes_accessed=4 * gram.size, transcendentals=0
        ),
    )(gram, start_basis)


def flip(value, axis, mask):
    size = lax.axis_size(axis)
    return lax.ppermute(value, axis, [(i, i ^ mask) for i in range(size)])


def gather_flips(block, axis):
    size, me = lax.axis_size(axis), lax.axis_index(axis)
    arrived = [block] + [flip(block, axis, mask) for mask in range(1, size)]
    stacked = jnp.zeros((size,) + block.shape, block.dtype)
    for mask, piece in enumerate(arrived):
        stacked = lax.dynamic_update_slice_in_dim(stacked, piece[None], me ^ mask, 0)
    return stacked.reshape((size * block.shape[0],) + block.shape[1:])


def scatter_sum_flips(parts, axis, wire):
    size, me = lax.axis_size(axis), lax.axis_index(axis)
    share = parts.shape[0] // size
    take = lambda owner: lax.dynamic_slice_in_dim(parts, owner * share, share, 0)
    total = take(me)
    for mask in range(1, size):
        total = total + flip(take(me ^ mask).astype(wire), axis, mask).astype(jnp.float32)
    return total


def sum_rows(value, beside):
    size, me = lax.axis_size("row"), lax.axis_index("row")
    core = me % 2
    half = value.shape[0] // 2
    take = lambda index: lax.dynamic_slice_in_dim(value, index * half, half, 0)
    pair = take(core) + flip(take(1 - core), "row", 1)
    arrived = [flip(pair, "row", mask) for mask in range(2, size, 2)]
    arrived, beside = lax.optimization_barrier((arrived, beside))
    total = pair
    for piece in arrived:
        total = total + piece
    back = flip(total, "row", 1)
    low = jnp.where(core == 0, total, back)
    high = jnp.where(core == 0, back, total)
    return jnp.concatenate([low, high], axis=0), beside


def dot32(a, b, dims=(((1,), (0,)), ((), ()))):
    return lax.dot_general(a, b, dims, precision=HIGHEST, preferred_element_type=jnp.float32)


ALONG = (((1,), (1,)), ((), ()))


BATCH = 8


def pick(value, j):
    return jnp.take_along_axis(value, jnp.full(value.shape, j, jnp.int32), axis=1)


def invert_block(work):
    n = work.shape[0]
    lane = lax.broadcasted_iota(jnp.int32, (BATCH, n), 1)
    down = lax.broadcasted_iota(jnp.int32, (n, n), 0)
    across = lax.broadcasted_iota(jnp.int32, (n, n), 1)
    level = lax.broadcasted_iota(jnp.int32, (BATCH, n), 0)

    def step(b, pivots):
        j = b * BATCH
        panel = work[pl.ds(pl.multiple_of(j, BATCH), BATCH), :]
        rows = [jnp.broadcast_to(panel[t : t + 1], (BATCH, n)) for t in range(BATCH)]
        entries = [[pick(rows[t], j + s) for s in range(t, BATCH)] for t in range(BATCH)]
        left = jnp.zeros((BATCH, n), jnp.float32)
        right = jnp.zeros((BATCH, n), jnp.float32)
        for t in range(BATCH):
            here = lane == j + t
            inverse = 1.0 / entries[t][0]
            pivots = jnp.where(here, entries[t][0], pivots)
            clean = jnp.where(here, 1.0, rows[t])
            for s in range(t + 1, BATCH):
                factor = entries[t][s - t] * inverse
                rows[s] = jnp.where(here, 0.0, rows[s]) - factor * clean
                for u in range(s, BATCH):
                    entries[s][u - s] = entries[s][u - s] - factor * entries[t][u - t]
            later = (lane > j + t) & (lane < j + BATCH)
            left = jnp.where(level == t, jnp.where(lane > j + t, rows[t] * inverse, 0.0), left)
            right = jnp.where(level == t, jnp.where(later, 0.0, clean), right)
        update = dot32(left, right, CONTRACT_ROWS)
        fresh = (across >= j) & (across < j + BATCH) & (down > across)
        work[...] = jnp.where(fresh, 0.0, work[...]) - update
        return pivots

    pivots = lax.fori_loop(0, n // BATCH, step, jnp.ones((BATCH, n), jnp.float32))
    unit = jnp.where(across < down, work[...], jnp.where(across == down, 1.0, 0.0))
    scale = jnp.sum(jnp.where(across == down, lax.rsqrt(pivots[:1]), 0.0), axis=1, keepdims=True)
    return unit * scale


def inverse_kernel(gram_ref, out_ref, work):
    half = work.shape[0]
    work[...] = gram_ref[:half, :half]
    inv11 = invert_block(work)
    a21 = gram_ref[half:, :half]
    l21 = dot32(a21, inv11, ALONG)
    work[...] = gram_ref[half:, half:] - dot32(l21, l21, ALONG)
    inv22 = invert_block(work)
    out_ref[:half, :half] = inv11
    out_ref[:half, half:] = jnp.zeros((half, half), jnp.float32)
    out_ref[half:, :half] = -dot32(inv22, dot32(l21, inv11))
    out_ref[half:, half:] = inv22


def inverse_factor(small_gram):
    half = small_gram.shape[0] // 2
    return pl.pallas_call(
        inverse_kernel,
        out_shape=jax.ShapeDtypeStruct(small_gram.shape, jnp.float32),
        scratch_shapes=[pltpu.VMEM((half, half), jnp.float32)],
        name="inverse_factor",
    )(small_gram)


def gram_kernel(y_ref, out_ref):
    @pl.when(pl.program_id(0) == 0)
    def _():
        out_ref[...] = jnp.zeros_like(out_ref)

    y = y_ref[...]
    out_ref[...] += lax.dot_general(y, y, CONTRACT_ROWS, preferred_element_type=jnp.float32)


def block_gram(y):
    tile = math.gcd(y.shape[0], 1024)
    size = y.shape[1]
    return pl.pallas_call(
        gram_kernel,
        grid=(y.shape[0] // tile,),
        in_specs=[pl.BlockSpec((tile, size), lambda i: (i, 0))],
        out_specs=pl.BlockSpec((size, size), lambda i: (0, 0)),
        out_shape=jax.ShapeDtypeStruct((size, size), jnp.float32),
        name="block_gram",
        cost_estimate=pl.CostEstimate(
            flops=2 * y.shape[0] * size * size, bytes_accessed=2 * y.size, transcendentals=0
        ),
    )(y)


def cross_kernel(slab_ref, y_ref, out_ref):
    @pl.when(pl.program_id(0) == 0)
    def _():
        out_ref[...] = jnp.zeros_like(out_ref)

    y = y_ref[...]
    slab = slab_ref[...]
    high = slab.astype(jnp.bfloat16)
    low = (slab - high.astype(jnp.float32)).astype(jnp.bfloat16)
    term = lambda a: lax.dot_general(a, y, CONTRACT_ROWS, preferred_element_type=jnp.float32)
    out_ref[...] += term(high) + term(low)


def cross_product(slab, y):
    tile = math.gcd(y.shape[0], 512)
    wide, size = slab.shape[1], y.shape[1]
    return pl.pallas_call(
        cross_kernel,
        grid=(y.shape[0] // tile,),
        in_specs=[
            pl.BlockSpec((tile, wide), lambda i: (i, 0)),
            pl.BlockSpec((tile, size), lambda i: (i, 0)),
        ],
        out_specs=pl.BlockSpec((wide, size), lambda i: (0, 0)),
        out_shape=jax.ShapeDtypeStruct((wide, size), jnp.float32),
        name="cross_product",
        cost_estimate=pl.CostEstimate(
            flops=4 * slab.size * size, bytes_accessed=4 * slab.size, transcendentals=0
        ),
    )(slab, y)


def shares_kernel(
    partial, slab, second_ref, gram_ref, crossed_ref,
    out1, in1, out2, in2, send1, recv1, send2, recv2,
    ys, y_send, y_recv, fwd_send, fwd_recv, tiles, tile_sem,
):
    r, c = lax.axis_index("row"), lax.axis_index("col")
    piece = second_ref.shape[0]
    half = piece // 2
    steps = 8
    part = piece * 4 // steps
    routes = ((1, 2), (2, 1))
    place = [c, c ^ 1, c ^ 2, c ^ 3]

    def remote(src, dst, send, recv, mask):
        return pltpu.make_async_remote_copy(
            src_ref=src, dst_ref=dst, send_sem=send, recv_sem=recv, device_id=(r, c ^ mask), device_id_type=MESH
        )

    def fetch(step):
        start = place[step // 2] * piece + (step % 2) * part
        return pltpu.make_async_copy(
            slab.at[pl.ds(pl.multiple_of(start, part), part), :], tiles.at[step % 2], tile_sem.at[step % 2]
        )

    fetch(0).start()
    fetch(1).start()
    barrier = pltpu.get_barrier_semaphore()
    for mask in (1, 2):
        pl.semaphore_signal(barrier, 1, device_id=(r, c ^ mask), device_id_type=MESH)
    pl.semaphore_wait(barrier, 2)

    def rows_of(owner, route):
        return partial[pl.ds(pl.multiple_of(owner * piece + route * half, half), half), :]

    def leg1(route, j):
        mask = routes[route][0]
        return remote(out1.at[route, j], in1.at[route, j], send1.at[route, j], recv1.at[route, j], mask)

    def leg2(route):
        mask = routes[route][1]
        return remote(out2.at[route], in2.at[route], send2.at[route], recv2.at[route], mask)

    for j in range(2):
        for route in range(2):
            owner = place[3] if j == 0 else place[routes[route][0]]
            out1[route, j] = rows_of(owner, route).astype(jnp.bfloat16)
            leg1(route, j).start()
    for route in range(2):
        leg1(route, 0).wait_recv()
        total = rows_of(place[routes[route][1]], route) + in1[route, 0].astype(jnp.float32)
        out2[route] = total.astype(jnp.bfloat16)
        leg2(route).start()
    for route in range(2):
        leg1(route, 1).wait_recv()
        leg2(route).wait_recv()
        total = rows_of(c, route) + in1[route, 1].astype(jnp.float32) + in2[route].astype(jnp.float32)
        second_ref[route * half : (route + 1) * half, :] = total
        ys[c, route * half : (route + 1) * half, :] = total.astype(jnp.bfloat16)

    def share(mask):
        return remote(ys.at[c], ys.at[c], y_send.at[mask - 1], y_recv.at[mask - 1], mask)

    def shared(mask):
        block = ys.at[c ^ mask]
        return remote(block, block, y_send.at[mask - 1], y_recv.at[mask - 1], mask)

    def forward(mask):
        low, to = (0, 2) if mask == 1 else (half, 1)
        block = ys.at[c ^ mask, low : low + half]
        return remote(block, block, fwd_send.at[mask - 1], fwd_recv.at[mask - 1], to)

    def forwarded(mask):
        low = 0 if mask == 1 else half
        block = ys.at[c ^ 3, low : low + half]
        return remote(block, block, fwd_send.at[mask - 1], fwd_recv.at[mask - 1], mask)

    def multiply(m):
        y = ys[place[m]]
        term = lax.dot_general(y, y, CONTRACT_ROWS, preferred_element_type=jnp.float32)
        gram_ref[...] = term if m == 0 else gram_ref[...] + term
        for step in (2 * m, 2 * m + 1):
            fetch(step).wait()
            tile = tiles[step % 2]
            high = tile.astype(jnp.bfloat16)
            low = (tile - high.astype(jnp.float32)).astype(jnp.bfloat16)
            rows = ys[place[m], (step % 2) * part : (step % 2 + 1) * part, :]
            dot = lambda a: lax.dot_general(a, rows, CONTRACT_ROWS, preferred_element_type=jnp.float32)
            value = dot(high) + dot(low)
            crossed_ref[...] = value if step == 0 else crossed_ref[...] + value
            if step + 2 < steps:
                fetch(step + 2).start()

    for mask in (1, 2):
        share(mask).start()
    multiply(0)
    for mask in (1, 2):
        shared(mask).wait_recv()
        forward(mask).start()
    multiply(1)
    multiply(2)
    for mask in (1, 2):
        forwarded(mask).wait_recv()
    multiply(3)
    for mask in (1, 2):
        share(mask).wait_send()
        forward(mask).wait_send()
    for route in range(2):
        leg1(route, 0).wait_send()
        leg1(route, 1).wait_send()
        leg2(route).wait_send()


def share_and_multiply(partial, slab):
    piece, width = partial.shape[0] // 4, partial.shape[1]
    half = piece // 2
    wide = slab.shape[1]
    dma = pltpu.SemaphoreType.DMA
    vmem = pl.BlockSpec(memory_space=pltpu.VMEM)
    return pl.pallas_call(
        shares_kernel,
        out_shape=(
            jax.ShapeDtypeStruct((piece, width), jnp.float32),
            jax.ShapeDtypeStruct((width, width), jnp.float32),
            jax.ShapeDtypeStruct((wide, width), jnp.float32),
        ),
        in_specs=[vmem, pl.BlockSpec(memory_space=pl.ANY)],
        out_specs=(vmem, vmem, vmem),
        scratch_shapes=[
            pltpu.VMEM((2, 2, half, width), jnp.bfloat16),
            pltpu.VMEM((2, 2, half, width), jnp.bfloat16),
            pltpu.VMEM((2, half, width), jnp.bfloat16),
            pltpu.VMEM((2, half, width), jnp.bfloat16),
            dma((2, 2)),
            dma((2, 2)),
            dma((2,)),
            dma((2,)),
            pltpu.VMEM((4, piece, width), jnp.bfloat16),
            dma((2,)),
            dma((2,)),
            dma((2,)),
            dma((2,)),
            pltpu.VMEM((2, half, wide), jnp.float32),
            dma((2,)),
        ],
        compiler_params=pltpu.CompilerParams(
            collective_id=1, has_side_effects=True, vmem_limit_bytes=48 << 20
        ),
        name="share_and_multiply",
        cost_estimate=pl.CostEstimate(
            flops=4 * slab.size * width, bytes_accessed=4 * slab.size, transcendentals=0
        ),
    )(partial, slab)


def finish_kernel(
    grams, crossed, inverse_ref, proj_ref,
    pair_in, pair_send, pair_recv, plane_in, plane_send, plane_recv, total, all_send, all_recv,
    mate_in, mate_send, mate_recv, sums, away, away_send, away_recv, work,
):
    rows, cols = lax.axis_size("row"), lax.axis_size("col")
    planes = rows // 2
    r, c = lax.axis_index("row"), lax.axis_index("col")
    z, core = lax.div(r, 2), lax.rem(r, 2)
    mate = (r + 1 - 2 * core, c)
    part = grams.shape[0] // (2 * cols)
    share = crossed.shape[0] // rows
    others = [(flip, mask) for mask in range(cols) for flip in range(2) if flip or mask]

    def remote(src, dst, send, recv, to):
        return pltpu.make_async_remote_copy(
            src_ref=src, dst_ref=dst, send_sem=send, recv_sem=recv, device_id=to, device_id_type=MESH
        )

    def level(step):
        return lax.rem(z + step, planes)

    def block(ref, column, side):
        return ref.at[pl.ds(pl.multiple_of((2 * column + side) * part, part), part), :]

    def piece(d, side):
        return crossed.at[pl.ds(pl.multiple_of((2 * d + side) * share, share), share), :]

    def beside(flip, mask):
        return (r + flip * (1 - 2 * core), c ^ mask)

    barrier = pltpu.get_barrier_semaphore()
    for step in range(1, planes):
        pl.semaphore_signal(barrier, 1, device_id=(2 * level(step) + core, c), device_id_type=MESH)
    for flip, mask in others:
        pl.semaphore_signal(barrier, 1, device_id=beside(flip, mask), device_id_type=MESH)
    pl.semaphore_wait(barrier, planes - 1 + len(others))

    pair = remote(block(grams, c, 1 - core), pair_in, pair_send, pair_recv, mate)
    pair.start()

    def to_mate(d):
        return remote(piece(d, 1 - core), mate_in.at[d], mate_send.at[d], mate_recv.at[d], mate)

    for d in range(planes):
        to_mate(d).start()

    pair.wait_recv()
    plane_in[z] = block(grams, c, core)[...] + pair_in[...]

    def to_plane(step):
        own = plane_in.at[z]
        return remote(own, own, plane_send.at[step], plane_recv.at[step], (2 * level(step) + core, c))

    def from_plane(step):
        there = plane_in.at[level(planes - step)]
        return remote(there, there, plane_send.at[step], plane_recv.at[step], mate)

    for step in range(1, planes):
        to_plane(step).start()
    for d in range(planes):
        to_mate(d).wait_recv()
        sums[d] = piece(d, core)[...] + mate_in[d]

    def to_owner(step):
        return remote(
            sums.at[level(step)], away.at[step], away_send.at[step], away_recv.at[step], (2 * level(step) + core, c)
        )

    for step in range(1, planes):
        to_owner(step).start()
    for step in range(1, planes):
        from_plane(step).wait_recv()
    value = plane_in[0]
    for d in range(1, planes):
        value = value + plane_in[d]
    block(total, c, core)[...] = value

    def to_other(n, flip, mask):
        own = block(total, c, core)
        return remote(own, own, all_send.at[n], all_recv.at[n], beside(flip, mask))

    def from_other(n, flip, mask):
        side = core + flip * (1 - 2 * core)
        there = block(total, c ^ mask, side)
        return remote(there, there, all_send.at[n], all_recv.at[n], mate)

    for n, (flip, mask) in enumerate(others):
        to_other(n, flip, mask).start()
    for n, (flip, mask) in enumerate(others):
        from_other(n, flip, mask).wait_recv()
    inverse_kernel(total, inverse_ref, work)
    mine = sums[z]
    for step in range(1, planes):
        to_owner(step).wait_recv()
        mine = mine + away[step]
    proj_ref[...] = dot32(inverse_ref[...], mine, ALONG)
    pair.wait_send()
    for d in range(planes):
        to_mate(d).wait_send()
    for step in range(1, planes):
        to_plane(step).wait_send()
        to_owner(step).wait_send()
    for n, (flip, mask) in enumerate(others):
        to_other(n, flip, mask).wait_send()


def finish(grams, crossed):
    rows, cols = lax.axis_size("row"), lax.axis_size("col")
    planes, width = rows // 2, grams.shape[0]
    part, share = width // (2 * cols), crossed.shape[0] // rows
    dma = pltpu.SemaphoreType.DMA
    f32 = lambda *shape: pltpu.VMEM(shape, jnp.float32)
    vmem = pl.BlockSpec(memory_space=pltpu.VMEM)
    return pl.pallas_call(
        finish_kernel,
        out_shape=(
            jax.ShapeDtypeStruct((width, width), jnp.float32),
            jax.ShapeDtypeStruct((width, share), jnp.float32),
        ),
        in_specs=[vmem, vmem],
        out_specs=(vmem, vmem),
        scratch_shapes=[
            f32(part, width), dma, dma,
            f32(planes, part, width), dma((planes,)), dma((planes,)),
            f32(width, width), dma((2 * cols - 1,)), dma((2 * cols - 1,)),
            f32(planes, share, width), dma((planes,)), dma((planes,)),
            f32(planes, share, width),
            f32(planes, share, width), dma((planes,)), dma((planes,)),
            f32(width // 2, width // 2),
        ],
        compiler_params=pltpu.CompilerParams(
            collective_id=2, has_side_effects=True, vmem_limit_bytes=24 << 20
        ),
        name="finish",
    )(grams, crossed)


def body(gram, start_basis, slab, order, modes):
    rows, cols = lax.axis_size("row"), lax.axis_size("col")
    partial = two_products(gram, start_basis)
    if cols == 4:
        second, grams, crossed = share_and_multiply(partial, slab)
        inverse, proj = finish(grams, crossed)
    else:
        second = scatter_sum_flips(partial, "col", jnp.bfloat16)
        block_second = gather_flips(second.astype(jnp.bfloat16), "col")
        small_gram, crossed = sum_rows(block_gram(block_second), cross_product(slab, block_second))
        crossed = lax.psum_scatter(crossed, "row", scatter_dimension=0, tiled=True)
        inverse = inverse_factor(small_gram)
        proj = dot32(inverse, crossed, ALONG)
    core_out = dot32(second, inverse, ALONG) * math.sqrt(order)
    count = rows * cols
    share = proj.shape[0] // count
    moved = lax.all_to_all(
        proj.reshape(count, share, proj.shape[1]), ("row", "col"), split_axis=0, concat_axis=0, tiled=True
    )
    moved = moved.reshape(rows, cols, share, proj.shape[1]).transpose(2, 1, 0, 3)
    return core_out, moved.reshape(share * modes, -1)


NMODE = 16


def solution(mesh):
    def whole(gram, start_basis, slab):
        order = gram.shape[0]
        inner = lambda g, s, w: body(g, s, w, order, NMODE)
        in_specs = (P("row", "col"), P(("row", "col"), None), P("row", "col"))
        out_specs = (P(("row", "col"), None), P(("row", "col"), None))
        return jax.shard_map(
            inner, mesh=mesh, in_specs=in_specs, out_specs=out_specs, check_vma=False
        )(gram, start_basis, slab)

    return whole
```
